128 devices in a mesh: dp: 32 (over z, y, core), mp: 4 (over x).
Axes of the slice: x: 4, y: 4, z: 4, core: 2. Of those that a mesh axis runs over, the one named last changes fastest.
Arguments:
- states: bfloat16 [128, 512, 1024], P('dp'), may hold values from -72 to 72
- lengths: int32 [128], P('dp'), may hold values from 64 to 512
- attn_in: bfloat16 [3, 1024, 1024], P(None, None, 'mp'), may hold values from -0.1875 to 0.1875
- attn_out: bfloat16 [1024, 1024], P('mp'), may hold values from -0.1875 to 0.1875
- attn_gain: float32 [1024], replicated, may hold values from 0.1 to 1.9
- ffn_up: bfloat16 [1024, 4096], P(None, 'mp'), may hold values from -0.1875 to 0.1875
- ffn_down: bfloat16 [4096, 1024], P('mp'), may hold values from -0.09375 to 0.09375
- ffn_gain: float32 [1024], replicated, may hold values from 0.1 to 1.9
- centroids: bfloat16 [65536, 1024], P(('dp', 'mp')), may hold values from -0.59765625 to 0.59765625
- assignment: int32 [128], replicated, may hold values from 0 to 65535
- list_place: int32 [65536], replicated, may hold values from 0 to 65535, as said below
Outputs:
- codes: float32 [128, 1024], P(('dp', 'mp'))
- lower: float32 [1024], replicated
- upper: float32 [1024], replicated
The draws below stay inside these ranges and needn't reach their ends.
Inputs may be any that keep to these rules, and one draw needn't show every extreme that they name: `list_place`: each number appears once.
All inputs are finite; a program needn't handle non-finite values.
Results may differ from the reference program's by a relative error of at most 0.0055.
Values may be sent and summed in bfloat16 or wider, within the bound.
A program may use at most 128 MiB of HBM per device.

```python
import jax
import jax.numpy as jnp
from jax import lax

D = 1024
HEADS = 16
HD = 64
FF = 4096
L = 512
DOC_DEV = 4
LISTS_DEV = 512
DOCS = 128
LISTS = 65536
N_MP = 4
DEVICES = 128


def draw_states(key, part):
    base = jax.random.truncated_normal(key, -6.0, 6.0, (DOCS, L, D), jnp.float32)
    return base.astype(jnp.bfloat16)


def routing_tables(key):
    joint_key = jax.random.fold_in(key, 11)
    perm_key, offset_key, within_key = jax.random.split(joint_key, 3)
    placement_table = jax.random.permutation(perm_key, LISTS).astype(jnp.int32)
    doc_ids = jnp.arange(DOCS, dtype=jnp.int32)
    holder = doc_ids // (DOC_DEV // N_MP)
    offset = jax.random.randint(offset_key, (DOCS,), 0, DEVICES).astype(jnp.int32)
    kind_of = doc_ids % 8
    offset = jnp.where(kind_of == 0, DEVICES // 2, jnp.where(kind_of == 1, 1, jnp.where(kind_of == 2, DEVICES - 1, offset))).astype(jnp.int32)
    owner = (holder + offset) % DEVICES
    within = jax.random.randint(within_key, (DOCS,), 0, LISTS_DEV).astype(jnp.int32)
    slot_of = (owner * LISTS_DEV + within).astype(jnp.int32)
    inverse = jnp.argsort(placement_table, stable=True).astype(jnp.int32)
    chosen = jnp.take(inverse, slot_of).astype(jnp.int32)
    return (placement_table, chosen)


def draw_list_place(key, part):
    placement_table, chosen = routing_tables(key)
    return placement_table


def draw_assignment(key, part):
    placement_table, chosen = routing_tables(key)
    return chosen


def touch_ends(drawn, own_key, smallest, top_value):
    extent = drawn.shape
    index_at = [jax.random.randint(jax.random.fold_in(own_key, axis), (), 0, extent[axis]) for axis in range(len(extent))]
    drawn = drawn.at[tuple(index_at)].set(smallest)
    longest = extent.index(max(extent))
    index_at[longest] = (index_at[longest] + 1) % extent[longest]
    return drawn.at[tuple(index_at)].set(top_value)


def shard_levels(stream_key, extent, cuts, low, largest):
    loudness = 1.0
    for position, shards_of in cuts:
        heights = jax.random.uniform(jax.random.fold_in(jax.random.fold_in(stream_key, 6), position), (shards_of,), jnp.float32, low / len(cuts), largest / len(cuts))
        loudness = loudness * jnp.repeat(jnp.exp(heights), extent[position] // shards_of).reshape((-1,) + (1,) * (len(extent) - 1 - position))
    return loudness


def noise(rng, extent, width, limit, cuts=(), held_as=jnp.bfloat16):
    level = shard_levels(rng, extent, cuts, -0.22, 0.18) if cuts else 1.0
    result = jax.random.normal(rng, extent, jnp.float32) * width * level
    return jnp.minimum(jnp.maximum(result, -limit), limit).astype(held_as)


def setup_inputs(seed: int = 0) -> dict:
    arg_keys = jax.random.split(jax.random.key(seed), 12)
    states = draw_states(jax.random.fold_in(arg_keys[11], 71), 0)
    lengths = touch_ends(jax.random.randint(arg_keys[1], (DOCS,), L // 8, L + 1), jax.random.fold_in(arg_keys[1], 1), L // 8, L).astype(jnp.int32)
    attn_in = noise(arg_keys[2], (3, D, D), D ** -0.5, 0.1875, ((2, 4),))
    attn_out = noise(arg_keys[3], (D, D), D ** -0.5, 0.1875, ((0, 4),))
    attn_gain = jnp.clip(1.0 + 0.18 * jax.random.normal(arg_keys[4], (D,), jnp.float32), 0.1, 1.9)
    ffn_up = noise(arg_keys[5], (D, FF), D ** -0.5, 0.1875, ((1, 4),))
    ffn_down = noise(arg_keys[6], (FF, D), FF ** -0.5, 0.09375, ((0, 4),))
    ffn_gain = jnp.clip(1.0 + 0.18 * jax.random.normal(arg_keys[7], (D,), jnp.float32), 0.1, 1.9)
    centroids = noise(arg_keys[8], (LISTS, D), 0.1, 0.59765625, ((0, 128),))
    assignment = draw_assignment(jax.random.fold_in(arg_keys[11], 71), 0)
    list_place = draw_list_place(jax.random.fold_in(arg_keys[11], 71), 0)
    return {"states": states, "lengths": lengths, "attn_in": attn_in, "attn_out": attn_out, "attn_gain": attn_gain, "ffn_up": ffn_up, "ffn_down": ffn_down, "ffn_gain": ffn_gain, "centroids": centroids, "assignment": assignment, "list_place": list_place}


norm_eps = 1e-12
range_eps = 1e-05

def norm_rows(values, gain):
    center = lax.optimization_barrier(jnp.mean(values, -1, keepdims=True))
    shifted = values - center
    spread = lax.optimization_barrier(jnp.mean(shifted * shifted, -1, keepdims=True))
    return shifted * lax.rsqrt(spread + norm_eps) * gain

def summed_rounded(partials):
    rounded = lax.optimization_barrier(partials.astype(jnp.bfloat16))
    return lax.optimization_barrier(jnp.sum(rounded.astype(jnp.float32), 0))

def reference(states, lengths, attn_in, attn_out, attn_gain, ffn_up, ffn_down, ffn_gain, centroids, assignment, list_place):
    head_group = D // N_MP
    unit_group = FF // N_MP

    def encode(item):
        span, length = item
        queries = jnp.dot(span, attn_in[0], preferred_element_type=jnp.float32).astype(jnp.bfloat16).reshape(L, HEADS, HD)
        keys_all = jnp.dot(span, attn_in[1], preferred_element_type=jnp.float32).astype(jnp.bfloat16).reshape(L, HEADS, HD)
        values_all = jnp.dot(span, attn_in[2], preferred_element_type=jnp.float32).astype(jnp.bfloat16).reshape(L, HEADS, HD)
        scores = jnp.einsum('qhc,khc->hqk', queries.astype(jnp.float32), keys_all.astype(jnp.float32)) * HD ** (-0.5)
        key_valid = jnp.arange(L, dtype=jnp.int32) < length
        scores = jnp.where(key_valid[None, None, :], scores, -1e+30)
        row_max = lax.optimization_barrier(jnp.max(scores, -1, keepdims=True))
        exp_scores = jnp.exp(scores - row_max)
        attn_probs = (exp_scores / lax.optimization_barrier(jnp.sum(exp_scores, -1, keepdims=True))).astype(jnp.bfloat16)
        context = jnp.einsum('hqk,khc->qhc', attn_probs.astype(jnp.float32), values_all.astype(jnp.float32)).astype(jnp.bfloat16).reshape(L, D)
        attn_parts = jnp.einsum('lgc,gcd->gld', context.reshape(L, N_MP, head_group).astype(jnp.float32), attn_out.reshape(N_MP, head_group, D).astype(jnp.float32))
        attn_total = summed_rounded(attn_parts)
        hidden = norm_rows(span.astype(jnp.float32) + attn_total, attn_gain).astype(jnp.bfloat16)
        inner_act = jax.nn.gelu(jnp.dot(hidden, ffn_up, preferred_element_type=jnp.float32), approximate=False).astype(jnp.bfloat16)
        ffn_parts = jnp.einsum('lgc,gcd->gld', inner_act.reshape(L, N_MP, unit_group).astype(jnp.float32), ffn_down.reshape(N_MP, unit_group, D).astype(jnp.float32))
        ffn_total = summed_rounded(ffn_parts)
        normed = norm_rows(hidden.astype(jnp.float32) + ffn_total, ffn_gain)
        masked = jnp.where(key_valid[:, None], normed, 0.0)
        return lax.optimization_barrier(jnp.sum(masked, 0)) / length.astype(jnp.float32)
    pooled = lax.map(encode, (states, lengths))
    slots = jnp.take(list_place, assignment).astype(jnp.int32)
    nearest = jnp.take(centroids, slots, axis=0).astype(jnp.float32)
    residual = pooled - nearest
    upper = lax.optimization_barrier(jnp.max(residual, 0))
    lower = lax.optimization_barrier(jnp.min(residual, 0))
    codes = (residual - lower) / (upper - lower + range_eps)
    return (codes, lower, upper)
```

```python
import jax
import jax.numpy as jnp
from jax import lax
from jax.experimental import pallas as pl
from jax.experimental.pallas import tpu as pltpu
from jax.sharding import PartitionSpec as P

MESH = pl.DeviceIdType.MESH
SEQ, WIDTH, GROUP = 512, 1024, 256
CUTS = 4
CHUNKS = 1 + 2 * CUTS
UNITS = WIDTH // CUTS
NORM_EPS, RANGE_EPS = 1e-12, 1e-05
COMM = True

STEPS = {}


def at(tau, kind, k):
    STEPS.setdefault(tau, []).append((kind, k))


for _k in range(CHUNKS):
    _b = (7 * _k) // 2
    at(max(0, _b), "x1", _k)
    at(_b + 2, "x2", _k)
    at(_b + 4, "a1", _k)
    at(_b + 7, "a2", _k)
    at(_b + 10, "co", _k)
for _t, _n in ((6, "n0"), (10, "n1"), (13, "n2"), (15, "n3"), (18, "n4")):
    at(_t, _n, 0)

DOC_SLOTS = 5
DOC_STEPS = 4 * DOC_SLOTS


def norm_rows(values, gain):
    center = jnp.mean(values, -1, keepdims=True)
    shifted = values - center
    spread = jnp.mean(shifted * shifted, -1, keepdims=True)
    return shifted * lax.rsqrt(spread + NORM_EPS) * gain


def gelu(v):
    return 0.5 * v * (1.0 + lax.erf(v * 0.7071067811865476))


def mm(a, b):
    return jnp.dot(a, b, preferred_element_type=jnp.float32)


def kernel(
    lens,
    states,
    w_in,
    w_out,
    gain1,
    w_up,
    w_down,
    gain2,
    cents,
    asg,
    places,
    codes_o,
    lower_o,
    upper_o,
    st,
    win,
    wout,
    up,
    down,
    cen,
    qs,
    ks,
    vs,
    cs,
    cr,
    hid,
    acc,
    nb0,
    nz,
    ny0,
    ny,
    nc0,
    nc,
    nx0,
    nx,
    es,
    er,
    lsem,
    wsem,
    ssem,
    rsem,
    asem,
    psem,
    s2sem,
    csem,
    nsem,
    esem,
):
    dp = lax.axis_index("dp")
    x = lax.axis_index("mp")
    c = lax.rem(dp, 2)
    y = lax.rem(dp // 2, 4)
    z = dp // 8

    def dev(x_, y_, z_, c_):
        return ((z_ * 4 + y_) * 2 + c_, x_)

    def plus(v, d):
        return lax.rem(v + (d + 4), 4)

    def peer(axis, d):
        if axis == "x":
            return dev(plus(x, d), y, z, c)
        if axis == "y":
            return dev(x, plus(y, d), z, c)
        if axis == "z":
            return dev(x, y, plus(z, d), c)
        return dev(x, y, z, 1 - c)

    def remote(src, dst, send, recv, to):
        return pltpu.make_async_remote_copy(
            src_ref=src, dst_ref=dst, send_sem=send, recv_sem=recv, device_id=to, device_id_type=MESH
        )

    def load_doc(i):
        return pltpu.make_async_copy(states.at[plus(x, i + 1)], st.at[i], lsem.at[i])

    load_win = pltpu.make_async_copy(w_in, win, lsem.at[4])
    load_wout = pltpu.make_async_copy(w_out, wout.at[0], lsem.at[5])
    load_up = [
        pltpu.make_async_copy(
            w_up.at[:, pl.ds(j * UNITS, UNITS)], up.at[0, j], lsem.at[8 + j]
        )
        for j in range(CUTS)
    ]
    load_down = [
        pltpu.make_async_copy(
            w_down.at[pl.ds(j * UNITS, UNITS), :], down.at[0, j], lsem.at[8 + CUTS + j]
        )
        for j in range(CUTS)
    ]
    load_cen = pltpu.make_async_copy(cents, cen, lsem.at[6])
    load_doc(0).start()
    load_win.start()
    for i in range(1, 4):
        load_doc(i).start()

    def chunk(k):
        if k == 0:
            return wout, (), w_out, 0, 0, 16, WIDTH
        j = (k - 1) // 2
        if k % 2:
            return up, (j,), w_up, 0, j * UNITS, 64, UNITS
        return down, (j,), w_down, j * UNITS, 0, 16, WIDTH

    def rows(k, cc, color, q, n=1):
        size = chunk(k)[5]
        start = cc * (8 * size) + color * (4 * size) + q * size
        return pl.ds(pl.multiple_of(start, size), n * size)

    def place(k, r, rws, cols=slice(None)):
        buf, mid = chunk(k)[:2]
        return buf.at[(r,) + mid + (rws, cols)]

    def mine(color):
        return y if color == 0 else z

    def step_x1(k, color, d):
        _, _, src, row0, col0, size, ncols = chunk(k)
        start = row0 + c * (8 * size) + color * (4 * size) + mine(color) * size
        piece = src.at[pl.ds(pl.multiple_of(start, size), size), pl.ds(col0, ncols)]
        dst = place(k, 3 if d > 0 else 1, rows(k, c, color, mine(color)))
        n = color * 2 + (0 if d > 0 else 1)
        return remote(piece, dst, wsem.at[k, n], ssem.at[k, n], peer("x", d))

    def step_x2(k, color):
        d = 1 if color == 0 else -1
        rws = rows(k, c, color, mine(color))
        return remote(
            place(k, 3 if d > 0 else 1, rws),
            place(k, 2, rws),
            wsem.at[k, 4 + color],
            ssem.at[k, 4 + color],
            peer("x", d),
        )

    def step_a1(k, color, d, arriving=False):
        q = plus(mine(color), -d) if arriving else mine(color)
        part = place(k, pl.ds(1, 3), rows(k, c, color, q))
        n = color * 4 + (0 if d > 0 else 1)
        return remote(
            part, part, asem.at[k, n], rsem.at[k, n], peer("yz"[color], d)
        )

    def step_a2(k, color, d, arriving=False):
        q = plus(mine(color), -2 * d if arriving else -d)
        size, ncols = chunk(k)[5:]
        half = 0 if d > 0 else 1
        if size >= 32:
            start = c * (8 * size) + color * (4 * size) + q * size + half * (size // 2)
            part = place(k, pl.ds(1, 3), pl.ds(pl.multiple_of(start, size // 2), size // 2))
        else:
            part = place(
                k, pl.ds(1, 3), rows(k, c, color, q), pl.ds(half * (ncols // 2), ncols // 2)
            )
        n = color * 4 + 2 + half
        return remote(
            part, part, asem.at[k, n], rsem.at[k, n], peer("yz"[color], d)
        )

    def step_co(k, color, arriving=False):
        part = place(k, pl.ds(1, 3), rows(k, 1 - c if arriving else c, color, 0, 4))
        return remote(part, part, s2sem.at[k, color], psem.at[k, color], peer("c", 1))

    both = [(color, d) for color in range(2) for d in (1, -1)]

    def near_z(d):
        rws = pl.ds(pl.multiple_of(plus(z, d) * 32, 32), 32)
        return remote(nb0.at[rws, :], nz.at[d - 1], nsem.at[0, 0, d - 1], nsem.at[1, 0, d - 1], peer("z", d))

    def near_y(d):
        rws = pl.ds(pl.multiple_of(plus(y, d) * 8, 8), 8)
        return remote(ny0.at[rws, :], ny.at[d - 1], nsem.at[0, 1, d - 1], nsem.at[1, 1, d - 1], peer("y", d))

    def near_c():
        return remote(nc0, nc, nsem.at[0, 2, 0], nsem.at[1, 2, 0], peer("c", 1))

    def near_x(d):
        return remote(nx0, nx.at[d - 1], nsem.at[0, 3, d - 1], nsem.at[1, 3, d - 1], peer("x", d))

    def near_first():
        load_cen.wait()
        ids = asg[...]
        hi = ids // 128
        lo = ids - hi * 128
        pick_hi = (hi == lax.broadcasted_iota(jnp.int32, (128, 512), 1)).astype(jnp.float32).astype(jnp.bfloat16)
        table = places[...]
        high = table // 256
        low = table - high * 256
        found = (
            mm(pick_hi, high.astype(jnp.float32).astype(jnp.bfloat16)) * 256.0
            + mm(pick_hi, low.astype(jnp.float32).astype(jnp.bfloat16))
        )
        lane = lax.broadcasted_iota(jnp.int32, (128, 128), 1)
        slot = jnp.sum(jnp.where(lane == lo, found, 0.0), -1, keepdims=True)
        first = ((dp * 4 + x) * 512).astype(jnp.float32)
        own = lax.broadcasted_iota(jnp.int32, (128, 512), 1).astype(jnp.float32)
        picker = (slot - first == own).astype(jnp.float32).astype(jnp.bfloat16)
        nb0[...] = mm(picker, cen[...]).astype(jnp.bfloat16)

    def event(kind, k):
        if kind == "x1":
            for color, d in both:
                step_x1(k, color, d).start()
        elif kind == "x2":
            step_x1(k, 0, 1).wait_recv()
            step_x2(k, 0).start()
            step_x1(k, 1, -1).wait_recv()
            step_x2(k, 1).start()
        elif kind == "a1":
            step_x1(k, 0, -1).wait_recv()
            step_x1(k, 1, 1).wait_recv()
            for color in range(2):
                step_x2(k, color).wait_recv()
            for color, d in both:
                step_a1(k, color, d).start()
        elif kind == "a2":
            for color, d in both:
                step_a1(k, color, d, True).wait_recv()
                step_a2(k, color, d).start()
        elif kind == "co":
            for color, d in both:
                step_a2(k, color, d, True).wait_recv()
            for color in range(2):
                step_co(k, color).start()
        elif kind == "n0":
            near_first()
            for d in (1, 2, 3):
                near_z(d).start()
        elif kind == "n1":
            total = nb0[pl.ds(pl.multiple_of(z * 32, 32), 32), :].astype(jnp.float32)
            for d in (1, 2, 3):
                near_z(d).wait_recv()
                total += nz[d - 1].astype(jnp.float32)
            ny0[...] = total
            for d in (1, 2, 3):
                near_y(d).start()
        elif kind == "n2":
            total = ny0[pl.ds(pl.multiple_of(y * 8, 8), 8), :]
            for d in (1, 2, 3):
                near_y(d).wait_recv()
                total += ny[d - 1]
            nc0[...] = total
            near_c().start()
        elif kind == "n3":
            near_c().wait_recv()
            nx0[...] = nc0[...] + nc[...]
            for d in (1, 2, 3):
                near_x(d).start()

    def flush(tau):
        if COMM:
            for kind, k in STEPS.get(tau, []):
                event(kind, k)

    def in_loop(i, slot):
        for ii in range(4):
            if STEPS.get(ii * DOC_SLOTS + slot):

                @pl.when(i == ii)
                def _():
                    flush(ii * DOC_SLOTS + slot)

    def send_ctx(i):
        return remote(cs.at[i], cr.at[3 - i], csem.at[0, i], csem.at[1, i], peer("x", i + 1))

    if COMM:
        barrier = pltpu.get_barrier_semaphore()
        peers = [peer(a, d) for a in "xyz" for d in (1, 2, 3)] + [peer("c", 1)]
        for p in peers:
            pl.semaphore_signal(barrier, inc=1, device_id=p, device_id_type=MESH)
        pl.semaphore_wait(barrier, len(peers))

    lane = lax.broadcasted_iota(jnp.int32, (256, 128), 1) < 64
    lane_all = lax.broadcasted_iota(jnp.int32, (SEQ, 128), 1) < 64

    def late_loads():
        load_cen.start()
        load_wout.start()
        for j in range(CUTS):
            load_up[j].start()
            load_down[j].start()

    @pl.loop(0, 4)
    def _(i):
        in_loop(i, 0)

        @pl.when(i == 0)
        def _():
            load_win.wait()
            late_loads()

        load_doc(i).wait()
        doc = st[i]
        q32 = mm(doc, win[0]) * 0.125
        for p in range(2):
            part = q32[:, p * 128 : p * 128 + 128]
            qs[2 * p] = jnp.where(lane_all, part, 0.0).astype(jnp.bfloat16)
            qs[2 * p + 1] = jnp.where(lane_all, 0.0, part).astype(jnp.bfloat16)
        ks[...] = mm(doc, win[1]).astype(jnp.bfloat16)
        v32 = mm(doc, win[2])
        for p in range(2):
            part = v32[:, p * 128 : p * 128 + 128]
            vs[2 * p] = jnp.where(lane_all, part, 1.0).astype(jnp.bfloat16)
            vs[2 * p + 1] = jnp.where(lane_all, 1.0, part).astype(jnp.bfloat16)
        bias = jnp.where(
            lax.broadcasted_iota(jnp.int32, (1, SEQ), 1) < lens[plus(x, i + 1)], 0.0, -1e30
        )
        for unit in range(4):
            p, qb = unit // 2, unit % 2
            in_loop(i, unit + 1)
            outs = []
            keys = ks[:, p * 128 : p * 128 + 128]
            for h in range(2):
                scores = lax.dot_general(
                    qs[2 * p + h, qb * 256 : qb * 256 + 256],
                    keys,
                    (((1,), (1,)), ((), ())),
                    preferred_element_type=jnp.float32,
                )
                scores = scores + bias
                e = jnp.exp(scores - jnp.max(scores, -1, keepdims=True)).astype(jnp.bfloat16)
                outs.append(mm(e, vs[2 * p + h]))
            top = jnp.where(lane, outs[0], outs[1])
            mass = pltpu.roll(jnp.where(lane, outs[1], outs[0]), 64, 1)
            cs[i, qb * 256 : qb * 256 + 256, p * 128 : p * 128 + 128] = (top / mass).astype(jnp.bfloat16)
        if COMM:
            for ii in range(3):

                @pl.when(i == ii)
                def _():
                    send_ctx(ii).start()

    tau = DOC_STEPS
    flush(tau)
    load_wout.wait()
    acc[...] = st[3].astype(jnp.float32) + mm(cs[3], wout[0])
    tau += 1
    flush(tau)
    if COMM:
        for color in range(2):
            step_co(0, color, True).wait_recv()
        for i in range(3):
            send_ctx(i).wait_recv()
    part = mm(cr[1], wout[1]) + mm(cr[2], wout[2]) + mm(cr[3], wout[3])
    hidden = norm_rows(acc[...] + part, gain1[...])
    hid[...] = hidden.astype(jnp.bfloat16)
    acc[...] = hid[...].astype(jnp.float32)

    def ffn(rs, js):
        for mb in range(2):
            rws = pl.ds(mb * 256, 256)
            h = hid[rws, :]
            total = acc[rws, :]
            for r in rs:
                for j in js:
                    act = gelu(mm(h, up[r, j])).astype(jnp.bfloat16)
                    total += mm(act, down[r, j])
            acc[rws, :] = total

    for jj in range(2):
        tau += 1
        flush(tau)
        for j in (2 * jj, 2 * jj + 1):
            load_up[j].wait()
            load_down[j].wait()
        ffn((0,), (2 * jj, 2 * jj + 1))
    last = max(STEPS)

    def arrive(j):
        for k in (1 + 2 * j, 2 + 2 * j):
            for color in range(2):
                step_co(k, color, True).wait_recv()

    for j in range(CUTS):
        need = max(t for t, ev in STEPS.items() if ("co", 2 + 2 * j) in ev)
        for _ in range(3):
            tau += 1
            flush(tau)
        while tau < need:
            tau += 1
            flush(tau)
        if COMM:
            arrive(j)
        ffn((1, 2, 3), (j,))
    assert tau >= last

    normed = norm_rows(acc[...], gain2[...])
    own_len = lens[x]
    live = lax.broadcasted_iota(jnp.int32, (SEQ, 1), 0) < own_len
    pooled = jnp.sum(jnp.where(live, normed, 0.0), 0, keepdims=True) / own_len.astype(jnp.float32)
    near = nx0[...]
    if COMM:
        for d in (1, 2, 3):
            near_x(d).wait_recv()
            near += nx[d - 1]
    mark = lax.broadcasted_iota(jnp.int32, (8, 1), 0) == c * 4 + x
    near = jnp.sum(jnp.where(mark, near, 0.0), 0, keepdims=True)
    flat = pooled - near
    for j in range(8):
        es[0, 0, j : j + 1, :] = flat[:, j * 128 : j * 128 + 128]
    residual = es[0, 0]
    es[0, 1] = -residual

    def extreme(stage, d):
        return remote(
            es.at[stage], er.at[stage, d - 1], esem.at[0, stage, d - 1], esem.at[1, stage, d - 1],
            peer("cxyz"[stage], d),
        )

    def reach(stage):
        return (1,) if stage == 0 else (1, 2, 3)

    best = jnp.concatenate([es[0, 0][None], es[0, 1][None]], 0)
    if COMM:
        for stage in range(4):
            if stage:
                es[stage] = best
            for d in reach(stage):
                extreme(stage, d).start()
            for d in reach(stage):
                extreme(stage, d).wait_recv()
                best = jnp.maximum(best, er[stage, d - 1])
    upper = best[0]
    lower = -best[1]
    upper_o[...] = upper
    lower_o[...] = lower
    codes_o[...] = (residual - lower) / (upper - lower + RANGE_EPS)

    if COMM:
        for k in range(CHUNKS):
            for color, d in both:
                step_x1(k, color, d).wait_send()
                step_a1(k, color, d).wait_send()
                step_a2(k, color, d).wait_send()
            for color in range(2):
                step_x2(k, color).wait_send()
                step_co(k, color).wait_send()
        for d in (1, 2, 3):
            near_z(d).wait_send()
            near_y(d).wait_send()
            near_x(d).wait_send()
        near_c().wait_send()
        for i in range(3):
            send_ctx(i).wait_send()
        for stage in range(4):
            for d in reach(stage):
                extreme(stage, d).wait_send()
    else:
        load_cen.wait()


def body(
    states,
    lengths,
    attn_in,
    attn_out,
    attn_gain,
    ffn_up,
    ffn_down,
    ffn_gain,
    centroids,
    assignment,
    list_place,
):
    hbm = pl.BlockSpec(memory_space=pl.ANY)
    vmem = pl.BlockSpec(memory_space=pltpu.VMEM)
    smem = pl.BlockSpec(memory_space=pltpu.SMEM)
    bf, f32 = jnp.bfloat16, jnp.float32
    tile = jax.ShapeDtypeStruct((8, 128), f32)
    dma = pltpu.SemaphoreType.DMA
    codes, lower, upper = pl.pallas_call(
        kernel,
        out_shape=(tile, tile, tile),
        in_specs=[smem, hbm, hbm, hbm, vmem, hbm, hbm, vmem, hbm, vmem, vmem],
        out_specs=(vmem, vmem, vmem),
        scratch_shapes=[
            pltpu.VMEM((4, SEQ, WIDTH), bf),
            pltpu.VMEM((3, WIDTH, GROUP), bf),
            pltpu.VMEM((4, GROUP, WIDTH), bf),
            pltpu.VMEM((4, CUTS, WIDTH, UNITS), bf),
            pltpu.VMEM((4, CUTS, UNITS, WIDTH), bf),
            pltpu.VMEM((512, WIDTH), bf),
            pltpu.VMEM((4, SEQ, 128), bf),
            pltpu.VMEM((SEQ, GROUP), bf),
            pltpu.VMEM((4, SEQ, 128), bf),
            pltpu.VMEM((4, SEQ, GROUP), bf),
            pltpu.VMEM((4, SEQ, GROUP), bf),
            pltpu.VMEM((SEQ, WIDTH), bf),
            pltpu.VMEM((SEQ, WIDTH), f32),
            pltpu.VMEM((128, WIDTH), bf),
            pltpu.VMEM((3, 32, WIDTH), bf),
            pltpu.VMEM((32, WIDTH), f32),
            pltpu.VMEM((3, 8, WIDTH), f32),
            pltpu.VMEM((8, WIDTH), f32),
            pltpu.VMEM((8, WIDTH), f32),
            pltpu.VMEM((8, WIDTH), f32),
            pltpu.VMEM((3, 8, WIDTH), f32),
            pltpu.VMEM((4, 2, 8, 128), f32),
            pltpu.VMEM((4, 3, 2, 8, 128), f32),
            dma((8 + 2 * CUTS,)),
            dma((CHUNKS, 6)),
            dma((CHUNKS, 6)),
            dma((CHUNKS, 8)),
            dma((CHUNKS, 8)),
            dma((CHUNKS, 2)),
            dma((CHUNKS, 2)),
            dma((2, 3)),
            dma((2, 4, 3)),
            dma((2, 4, 3)),
        ],
        compiler_params=pltpu.CompilerParams(
            vmem_limit_bytes=60 * 2**20,
            **(dict(collective_id=0, has_side_effects=True) if COMM else {}),
        ),
        name="encode",
    )(
        lengths,
        states,
        attn_in,
        attn_out,
        attn_gain.reshape(1, WIDTH),
        ffn_up,
        ffn_down,
        ffn_gain.reshape(1, WIDTH),
        centroids,
        assignment.reshape(128, 1),
        list_place.reshape(512, 128),
    )
    return codes.reshape(1, WIDTH), lower.reshape(WIDTH), upper.reshape(WIDTH)


def solution(mesh):
    placed = (
        P("dp", None, None),
        P("dp"),
        P(None, None, "mp"),
        P("mp", None),
        P(),
        P(None, "mp"),
        P("mp", None),
        P(),
        P(("dp", "mp"), None),
        P(),
        P(),
    )
    return jax.shard_map(
        body,
        mesh=mesh,
        in_specs=placed,
        out_specs=(P(("dp", "mp"), None), P(), P()),
        check_vma=False,
    )
```

```python
import jax
import jax.numpy as jnp
from jax import lax
from jax.experimental import pallas as pl
from jax.experimental.pallas import tpu as pltpu
from jax.sharding import PartitionSpec as P

MESH = pl.DeviceIdType.MESH
SEQ, WIDTH, GROUP = 512, 1024, 256
CUTS = 4
QB = 1
CHUNKS = 1 + 2 * CUTS
UNITS = WIDTH // CUTS
NORM_EPS, RANGE_EPS = 1e-12, 1e-05
COMM = True

DOC_ORDER = (2, 1, 3, 0)
CTX_SLOT = (3, 2, 1)

STEPS = {
    "u00": (("x1", 0, 0), ("x1", 1, 0), ("x1", 2, 0), ("n0", 0, 0),),
    "u01": (("x1", 3, 0), ("x1", 4, 0), ("x1", 5, 0),),
    "q1": (("a1", 0, 0),),
    "u10": (("x2", 0, 0), ("x1", 6, 0), ("x1", 7, 0), ("x1", 8, 0),),
    "u11": (("a1", 1, 0), ("a1", 2, 0), ("n1", 0, 0), ("x2", 1, 0), ("x2", 2, 0),),
    "q2": (("a2", 0, 0),),
    "u21": (("a2", 1, 0), ("a1", 3, 0), ("a1", 4, 0), ("x2", 4, 0),),
    "q3": (("a2", 2, 0), ("a1", 5, 0), ("x2", 5, 0), ("x2", 3, 0),),
    "u30": (("co", 0, 0), ("co", 1, 0), ("n2", 0, 0),),
    "u31": (("a1", 0, 1), ("a2", 3, 0),),
    "o0": (("a2", 4, 0), ("a1", 6, 0), ("a1", 7, 0), ("co", 2, 0), ("x2", 6, 0), ("x2", 7, 0),),
    "o1": (("a2", 5, 0), ("a1", 8, 0), ("n3", 0, 0), ("a2", 0, 1), ("co", 3, 0), ("co", 4, 0), ("a1", 1, 1), ("a2", 6, 0), ("a1", 2, 1), ("x2", 8, 0), ("a2", 7, 0), ("co", 5, 0), ("a2", 8, 0), ("a1", 4, 1), ("co", 0, 1), ("a1", 5, 1), ("a2", 1, 1), ("a1", 3, 1), ("co", 6, 0), ("a1", 6, 1),),
    "f00": (("a2", 2, 1), ("a1", 7, 1), ("co", 7, 0), ("co", 8, 0),),
    "f01": (("a2", 4, 1), ("a2", 5, 1), ("a1", 8, 1),),
    "f10": (("a2", 3, 1), ("co", 1, 1),),
    "f11": (("a2", 6, 1),),
    "g00": (("co", 2, 1),),
    "g01": (("a2", 7, 1),),
    "g10": (("co", 4, 1), ("co", 5, 1),),
    "g11": (("a2", 8, 1), ("co", 3, 1),),
    "g20": (("co", 6, 1),),
    "g30": (("co", 7, 1),),
    "h00": (("co", 8, 1),),
}
STEPS_OF = {ev: n for n, ev in enumerate(e for evs in STEPS.values() for e in evs)}


def norm_rows(values, gain):
    center = jnp.mean(values, -1, keepdims=True)
    shifted = values - center
    spread = jnp.mean(shifted * shifted, -1, keepdims=True)
    return shifted * lax.rsqrt(spread + NORM_EPS) * gain


def gelu(v):
    return 0.5 * v * (1.0 + lax.erf(v * 0.7071067811865476))


def mm(a, b):
    return jnp.dot(a, b, preferred_element_type=jnp.float32)


def mm_rows(a, b):
    return lax.dot_general(a, b, (((0,), (0,)), ((), ())), preferred_element_type=jnp.float32)


def kernel(
    lens,
    states,
    w_in,
    w_out,
    gain1,
    w_up,
    w_down,
    gain2,
    cents,
    asg,
    places,
    res_o,
    ext_o,
    st,
    win,
    wout,
    up,
    down,
    cen,
    qs,
    ks,
    vs,
    cs,
    cr,
    hid,
    acc,
    nb0,
    nz,
    ny0,
    ny,
    nc0,
    nc,
    nx0,
    nx,
    es,
    er,
    lsem,
    wsem,
    ssem,
    rsem,
    asem,
    psem,
    s2sem,
    csem,
    nsem,
    esem,
):
    dp = lax.axis_index("dp")
    x = lax.axis_index("mp")
    c = lax.rem(dp, 2)
    y = lax.rem(dp // 2, 4)
    z = dp // 8

    def dev(x_, y_, z_, c_):
        return ((z_ * 4 + y_) * 2 + c_, x_)

    def plus(v, d):
        return lax.rem(v + (d + 4), 4)

    def peer(axis, d):
        if axis == "x":
            return dev(plus(x, d), y, z, c)
        if axis == "y":
            return dev(x, plus(y, d), z, c)
        if axis == "z":
            return dev(x, y, plus(z, d), c)
        return dev(x, y, z, 1 - c)

    def group(stage, n):
        if stage == 0:
            return dev(plus(x, n // 2), y, z, lax.rem(c + n, 2))
        return peer("xyz"[stage], n)

    def remote(src, dst, send, recv, to):
        return pltpu.make_async_remote_copy(
            src_ref=src, dst_ref=dst, send_sem=send, recv_sem=recv, device_id=to, device_id_type=MESH
        )

    def turn(i):
        return lax.rem(x + (2 + 3 * i + 3 * (i // 2) + 2 * (i // 3)), 4)

    def load_doc(i):
        return pltpu.make_async_copy(states.at[turn(i)], st.at[i], lsem.at[i])

    load_win = pltpu.make_async_copy(w_in, win, lsem.at[4])
    load_wout = pltpu.make_async_copy(w_out, wout.at[0], lsem.at[5])
    load_up = [
        pltpu.make_async_copy(
            w_up.at[:, pl.ds(j * UNITS, UNITS)], up.at[0, j], lsem.at[8 + j]
        )
        for j in range(CUTS)
    ]
    load_down = [
        pltpu.make_async_copy(
            w_down.at[pl.ds(j * UNITS, UNITS), :], down.at[0, j], lsem.at[8 + CUTS + j]
        )
        for j in range(CUTS)
    ]
    load_cen = pltpu.make_async_copy(cents, cen, lsem.at[6])
    load_doc(0).start()
    load_win.start()
    load_cen.start()
    for i in range(1, 4):
        load_doc(i).start()
    load_wout.start()
    for j in range(CUTS):
        load_up[j].start()
        load_down[j].start()

    def chunk(k):
        if k == 0:
            return wout, (), w_out, 0, 0, 16, WIDTH
        j = (k - 1) // 2
        if k % 2:
            return up, (j,), w_up, 0, j * UNITS, 64, UNITS
        return down, (j,), w_down, j * UNITS, 0, 16, WIDTH

    def rows(k, cc, color, q, n=1):
        size = chunk(k)[5]
        start = cc * (8 * size) + color * (4 * size) + q * size
        return pl.ds(pl.multiple_of(start, size), n * size)

    def place(k, r, rws, cols=slice(None)):
        buf, mid = chunk(k)[:2]
        return buf.at[(r,) + mid + (rws, cols)]

    def mine(color):
        return y if color == 0 else z

    def step_x1(k, color, d):
        _, _, src, row0, col0, size, ncols = chunk(k)
        start = row0 + c * (8 * size) + color * (4 * size) + mine(color) * size
        piece = src.at[pl.ds(pl.multiple_of(start, size), size), pl.ds(col0, ncols)]
        dst = place(k, 2 if d > 0 else 1, rows(k, c, color, mine(color)))
        n = color * 2 + (0 if d > 0 else 1)
        return remote(piece, dst, wsem.at[k, n], ssem.at[k, n], peer("x", d))

    def step_x2(k, color):
        d = 1 if color == 0 else -1
        rws = rows(k, c, color, mine(color))
        return remote(
            place(k, 2 if d > 0 else 1, rws),
            place(k, 3, rws),
            wsem.at[k, 4 + color],
            ssem.at[k, 4 + color],
            peer("x", d),
        )

    def span(p):
        return pl.ds(1, 2) if p == 0 else pl.ds(3, 1)

    def step_a1(k, p, color, d, arriving=False):
        q = plus(mine(color), -d) if arriving else mine(color)
        part = place(k, span(p), rows(k, c, color, q))
        n = color * 4 + (0 if d > 0 else 1)
        return remote(
            part, part, asem.at[k, p, n], rsem.at[k, p, n], peer("yz"[color], d)
        )

    def step_a2(k, p, color, d, arriving=False):
        q = plus(mine(color), -2 * d if arriving else -d)
        size, ncols = chunk(k)[5:]
        half = 0 if d > 0 else 1
        if size >= 32:
            start = c * (8 * size) + color * (4 * size) + q * size + half * (size // 2)
            part = place(k, span(p), pl.ds(pl.multiple_of(start, size // 2), size // 2))
        else:
            part = place(
                k, span(p), rows(k, c, color, q), pl.ds(half * (ncols // 2), ncols // 2)
            )
        n = color * 4 + 2 + half
        return remote(
            part, part, asem.at[k, p, n], rsem.at[k, p, n], peer("yz"[color], d)
        )

    def step_co(k, p, color, arriving=False):
        part = place(k, span(p), rows(k, 1 - c if arriving else c, color, 0, 4))
        return remote(part, part, s2sem.at[k, p, color], psem.at[k, p, color], peer("c", 1))

    both = [(color, d) for color in range(2) for d in (1, -1)]

    def near_z(d):
        rws = pl.ds(pl.multiple_of(plus(z, d) * 32, 32), 32)
        return remote(nb0.at[rws, :], nz.at[d - 1], nsem.at[0, 0, d - 1], nsem.at[1, 0, d - 1], peer("z", d))

    def near_y(d):
        rws = pl.ds(pl.multiple_of(plus(y, d) * 8, 8), 8)
        return remote(ny0.at[rws, :], ny.at[d - 1], nsem.at[0, 1, d - 1], nsem.at[1, 1, d - 1], peer("y", d))

    def near_c():
        return remote(nc0, nc, nsem.at[0, 2, 0], nsem.at[1, 2, 0], peer("c", 1))

    def near_x(d):
        return remote(nx0, nx.at[d - 1], nsem.at[0, 3, d - 1], nsem.at[1, 3, d - 1], peer("x", d))

    def near_first():
        load_cen.wait()
        ids = asg[...]
        hi = ids // 128
        lo = ids - hi * 128
        slots = lax.broadcasted_iota(jnp.int32, (512, 128), 0)
        pick_hi = (hi == slots).astype(jnp.float32).astype(jnp.bfloat16)
        table = places[...]
        high = table // 256
        low = table - high * 256
        found = (
            mm_rows(high.astype(jnp.float32).astype(jnp.bfloat16), pick_hi) * 256.0
            + mm_rows(low.astype(jnp.float32).astype(jnp.bfloat16), pick_hi)
        )
        lanes = lax.broadcasted_iota(jnp.int32, (128, 128), 0)
        slot = jnp.sum(jnp.where(lanes == lo, found, 0.0), 0, keepdims=True)
        first = ((dp * 4 + x) * 512).astype(jnp.float32)
        picker = (slot - first == slots.astype(jnp.float32)).astype(jnp.float32).astype(jnp.bfloat16)
        nb0[...] = mm_rows(picker, cen[...]).astype(jnp.bfloat16)

    def event(kind, k, p):
        if kind == "x1":
            for color, d in both:
                step_x1(k, color, d).start()
        elif kind == "x2":
            before = STEPS_OF[("x2", k, 0)] < STEPS_OF[("a1", k, 0)]
            for color, d in ((0, 1), (1, -1)):
                if before:
                    step_x1(k, color, d).wait_recv()
                step_x2(k, color).start()
        elif kind == "a1":
            if p == 0:
                step_x1(k, 0, -1).wait_recv()
                step_x1(k, 1, 1).wait_recv()
                if STEPS_OF[("x2", k, 0)] > STEPS_OF[("a1", k, 0)]:
                    step_x1(k, 0, 1).wait_recv()
                    step_x1(k, 1, -1).wait_recv()
            else:
                for color in range(2):
                    step_x2(k, color).wait_recv()
            for color, d in both:
                step_a1(k, p, color, d).start()
        elif kind == "a2":
            for color, d in both:
                step_a1(k, p, color, d, True).wait_recv()
                step_a2(k, p, color, d).start()
        elif kind == "co":
            for color, d in both:
                step_a2(k, p, color, d, True).wait_recv()
            for color in range(2):
                step_co(k, p, color).start()
        elif kind == "n0":
            for d in (1, 2, 3):
                near_z(d).start()
        elif kind == "n1":
            total = nb0[pl.ds(pl.multiple_of(z * 32, 32), 32), :].astype(jnp.float32)
            for d in (1, 2, 3):
                near_z(d).wait_recv()
                total += nz[d - 1].astype(jnp.float32)
            ny0[...] = total
            for d in (1, 2, 3):
                near_y(d).start()
        elif kind == "n2":
            total = ny0[pl.ds(pl.multiple_of(y * 8, 8), 8), :]
            for d in (1, 2, 3):
                near_y(d).wait_recv()
                total += ny[d - 1]
            nc0[...] = total
            near_c().start()
        elif kind == "n3":
            near_c().wait_recv()
            nx0[...] = nc0[...] + nc[...]
            for d in (1, 2, 3):
                near_x(d).start()

    def flush(tau):
        if COMM:
            for kind, k, p in STEPS.get(tau, ()):
                event(kind, k, p)

    def in_loop(i, slot):
        for ii in range(4):
            tau = f"q{ii + 1}" if slot == 2 else f"u{ii}{slot}"
            if STEPS.get(tau):

                @pl.when(i == ii)
                def _():
                    flush(tau)

    def send_ctx(i, p):
        cols = pl.ds(p * 128, 128)
        return remote(
            cs.at[i, :, cols],
            cr.at[CTX_SLOT[i], :, cols],
            csem.at[0, i, p],
            csem.at[1, i, p],
            peer("x", DOC_ORDER[i]),
        )

    if COMM:
        barrier = pltpu.get_barrier_semaphore()
        peers = [group(0, n) for n in range(1, 8)] + [peer(a, d) for a in "yz" for d in (1, 2, 3)]
        for p in peers:
            pl.semaphore_signal(barrier, inc=1, device_id=p, device_id_type=MESH)

    lane = lax.broadcasted_iota(jnp.int32, (SEQ // QB, 128), 1) < 64
    lane_all = lax.broadcasted_iota(jnp.int32, (SEQ, 128), 1) < 64

    def project(i):
        load_doc(i).wait()
        doc = st[i]
        q32 = mm(doc, win[0]) * 0.125
        for p in range(2):
            part = q32[:, p * 128 : p * 128 + 128]
            qs[2 * p] = jnp.where(lane_all, part, 0.0).astype(jnp.bfloat16)
            qs[2 * p + 1] = jnp.where(lane_all, 0.0, part).astype(jnp.bfloat16)
        ks[...] = mm(doc, win[1]).astype(jnp.bfloat16)
        v32 = mm(doc, win[2])
        for p in range(2):
            part = v32[:, p * 128 : p * 128 + 128]
            vs[2 * p] = jnp.where(lane_all, part, 1.0).astype(jnp.bfloat16)
            vs[2 * p + 1] = jnp.where(lane_all, 1.0, part).astype(jnp.bfloat16)
    load_win.wait()
    project(0)
    if COMM:
        near_first()
        pl.semaphore_wait(barrier, len(peers))

    @pl.loop(0, 4)
    def _(i):
        bias = jnp.where(
            lax.broadcasted_iota(jnp.int32, (1, SEQ), 1) < lens[turn(i)], 0.0, -1e30
        )
        for p in range(2):
            in_loop(i, p)
            keys = ks[:, p * 128 : p * 128 + 128]
            for qb in range(QB):
                outs = []
                rws = pl.ds(qb * (SEQ // QB), SEQ // QB)
                for h in range(2):
                    scores = lax.dot_general(
                        qs[2 * p + h, rws],
                        keys,
                        (((1,), (1,)), ((), ())),
                        preferred_element_type=jnp.float32,
                    )
                    scores = scores + bias
                    e = jnp.exp(scores - jnp.max(scores, -1, keepdims=True)).astype(jnp.bfloat16)
                    outs.append(mm(e, vs[2 * p + h]))
                top = jnp.where(lane, outs[0], outs[1])
                mass = pltpu.roll(jnp.where(lane, outs[1], outs[0]), 64, 1)
                cs[i, rws, p * 128 : p * 128 + 128] = (top / mass).astype(jnp.bfloat16)
            if COMM:
                for ii in range(3):

                    @pl.when(i == ii)
                    def _():
                        send_ctx(ii, p).start()

        in_loop(i, 2)

        @pl.when(i < 3)
        def _():
            project(i + 1)

    def arrive(k, p):
        if COMM:
            for color in range(2):
                step_co(k, p, color, True).wait_recv()

    flush("o0")
    load_wout.wait()
    acc[...] = st[3].astype(jnp.float32) + mm(cs[3], wout[0])
    flush("o1")
    arrive(0, 0)
    arrive(0, 1)
    if COMM:
        for i in range(3):
            for p in range(2):
                send_ctx(i, p).wait_recv()
    part = mm(cr[1], wout[1]) + mm(cr[2], wout[2]) + mm(cr[3], wout[3])
    hidden = norm_rows(acc[...] + part, gain1[...])
    hid[...] = hidden.astype(jnp.bfloat16)
    acc[...] = hid[...].astype(jnp.float32)

    def ffn(parts, between):
        for mb in range(2):
            if mb:
                flush(between)
            rws = pl.ds(mb * 256, 256)
            h = hid[rws, :]
            total = acc[rws, :]
            for r, j in parts:
                act = gelu(mm(h, up[r, j])).astype(jnp.bfloat16)
                total += mm(act, down[r, j])
            acc[rws, :] = total

    for n in range(CUTS // 2):
        flush(f"f{n}0")
        for j in (2 * n, 2 * n + 1):
            load_up[j].wait()
            load_down[j].wait()
        ffn(((0, 2 * n), (0, 2 * n + 1)), f"f{n}1")
    for j in range(CUTS):
        flush(f"g{j}0")
        arrive(1 + 2 * j, 0)
        arrive(2 + 2 * j, 0)
        ffn(((1, j), (2, j)), f"g{j}1")
    for n in range(CUTS // 2):
        flush(f"h{n}0")
        for k in range(1 + 4 * n, 5 + 4 * n):
            arrive(k, 1)
        ffn(((3, 2 * n), (3, 2 * n + 1)), f"h{n}1")
    flush("end")

    normed = norm_rows(acc[...], gain2[...])
    own_len = lens[x]
    live = lax.broadcasted_iota(jnp.int32, (SEQ, 1), 0) < own_len
    pooled = jnp.sum(jnp.where(live, normed, 0.0), 0, keepdims=True) / own_len.astype(jnp.float32)
    near = nx0[...]
    if COMM:
        for d in (1, 2, 3):
            near_x(d).wait_recv()
            near += nx[d - 1]
    mark = lax.broadcasted_iota(jnp.int32, (8, 1), 0) == c * 4 + x
    near = jnp.sum(jnp.where(mark, near, 0.0), 0, keepdims=True)
    flat = pooled - near
    for j in range(8):
        es[0, 0, j : j + 1, :] = flat[:, j * 128 : j * 128 + 128]
    residual = es[0, 0]
    es[0, 1] = -residual

    def extreme(stage, n):
        return remote(
            es.at[stage], er.at[stage, n - 1], esem.at[0, stage, n - 1], esem.at[1, stage, n - 1],
            group(stage, n),
        )

    def reach(stage):
        return range(1, 8 if stage == 0 else 4)

    def sent(k):
        for color, d in both:
            step_x1(k, color, d).wait_send()
            for p in range(2):
                step_a1(k, p, color, d).wait_send()
                step_a2(k, p, color, d).wait_send()
        for color in range(2):
            step_x2(k, color).wait_send()
            for p in range(2):
                step_co(k, p, color).wait_send()

    best = jnp.concatenate([es[0, 0][None], es[0, 1][None]], 0)
    if COMM:
        for stage in range(3):
            if stage:
                es[stage] = best
            for d in reach(stage):
                extreme(stage, d).start()
            for k in range(3 * stage, 3 * stage + 3):
                sent(k)
            for d in reach(stage):
                extreme(stage, d).wait_recv()
                best = jnp.maximum(best, er[stage, d - 1])
    res_o[...] = residual
    ext_o[...] = best

    if COMM:
        for d in (1, 2, 3):
            near_z(d).wait_send()
            near_y(d).wait_send()
            near_x(d).wait_send()
        near_c().wait_send()
        for i in range(3):
            for p in range(2):
                send_ctx(i, p).wait_send()
        for stage in range(3):
            for d in reach(stage):
                extreme(stage, d).wait_send()
    else:
        load_cen.wait()


def finish(res, ext, codes_o, lower_o, upper_o):
    upper = ext[0]
    lower = -ext[1]
    upper_o[...] = upper
    lower_o[...] = lower
    codes_o[...] = (res[...] - lower) / (upper - lower + RANGE_EPS)


def body(
    states,
    lengths,
    attn_in,
    attn_out,
    attn_gain,
    ffn_up,
    ffn_down,
    ffn_gain,
    centroids,
    assignment,
    list_place,
):
    hbm = pl.BlockSpec(memory_space=pl.ANY)
    vmem = pl.BlockSpec(memory_space=pltpu.VMEM)
    smem = pl.BlockSpec(memory_space=pltpu.SMEM)
    bf, f32 = jnp.bfloat16, jnp.float32
    tile = jax.ShapeDtypeStruct((8, 128), f32)
    dma = pltpu.SemaphoreType.DMA
    residual, extremes = pl.pallas_call(
        kernel,
        out_shape=(tile, jax.ShapeDtypeStruct((2, 8, 128), f32)),
        in_specs=[smem, hbm, hbm, hbm, vmem, hbm, hbm, vmem, hbm, vmem, vmem],
        out_specs=(vmem, vmem),
        scratch_shapes=[
            pltpu.VMEM((4, SEQ, WIDTH), bf),
            pltpu.VMEM((3, WIDTH, GROUP), bf),
            pltpu.VMEM((4, GROUP, WIDTH), bf),
            pltpu.VMEM((4, CUTS, WIDTH, UNITS), bf),
            pltpu.VMEM((4, CUTS, UNITS, WIDTH), bf),
            pltpu.VMEM((512, WIDTH), bf),
            pltpu.VMEM((4, SEQ, 128), bf),
            pltpu.VMEM((SEQ, GROUP), bf),
            pltpu.VMEM((4, SEQ, 128), bf),
            pltpu.VMEM((4, SEQ, GROUP), bf),
            pltpu.VMEM((4, SEQ, GROUP), bf),
            pltpu.VMEM((SEQ, WIDTH), bf),
            pltpu.VMEM((SEQ, WIDTH), f32),
            pltpu.VMEM((128, WIDTH), bf),
            pltpu.VMEM((3, 32, WIDTH), bf),
            pltpu.VMEM((32, WIDTH), f32),
            pltpu.VMEM((3, 8, WIDTH), f32),
            pltpu.VMEM((8, WIDTH), f32),
            pltpu.VMEM((8, WIDTH), f32),
            pltpu.VMEM((8, WIDTH), f32),
            pltpu.VMEM((3, 8, WIDTH), f32),
            pltpu.VMEM((3, 2, 8, 128), f32),
            pltpu.VMEM((3, 7, 2, 8, 128), f32),
            dma((8 + 2 * CUTS,)),
            dma((CHUNKS, 6)),
            dma((CHUNKS, 6)),
            dma((CHUNKS, 2, 8)),
            dma((CHUNKS, 2, 8)),
            dma((CHUNKS, 2, 2)),
            dma((CHUNKS, 2, 2)),
            dma((2, 3, 2)),
            dma((2, 4, 3)),
            dma((2, 3, 7)),
        ],
        compiler_params=pltpu.CompilerParams(
            vmem_limit_bytes=60 * 2**20,
            **(dict(collective_id=0, has_side_effects=True) if COMM else {}),
        ),
        name="encode",
    )(
        lengths,
        states,
        attn_in,
        attn_out,
        attn_gain.reshape(1, WIDTH),
        ffn_up,
        ffn_down,
        ffn_gain.reshape(1, WIDTH),
        centroids,
        assignment.reshape(1, 128),
        list_place.reshape(512, 128),
    )
    codes, lower, upper = pl.pallas_call(
        finish,
        out_shape=(tile, tile, tile),
        in_specs=[vmem, vmem],
        out_specs=(vmem, vmem, vmem),
        name="finish",
    )(residual, extremes)
    return codes.reshape(1, WIDTH), lower.reshape(WIDTH), upper.reshape(WIDTH)


def solution(mesh):
    placed = (
        P("dp", None, None),
        P("dp"),
        P(None, None, "mp"),
        P("mp", None),
        P(),
        P(None, "mp"),
        P("mp", None),
        P(),
        P(("dp", "mp"), None),
        P(),
        P(),
    )
    return jax.shard_map(
        body,
        mesh=mesh,
        in_specs=placed,
        out_specs=(P(("dp", "mp"), None), P(), P()),
        check_vma=False,
    )
```

```python
import jax
import jax.numpy as jnp
from jax import lax
from jax.experimental import pallas as pl
from jax.experimental.pallas import tpu as pltpu
from jax.sharding import PartitionSpec as P

MESH = pl.DeviceIdType.MESH
SEQ, WIDTH, GROUP = 512, 1024, 256
CUTS = 4
QB = 1
CHUNKS = 1 + 2 * CUTS
UNITS = WIDTH // CUTS
NORM_EPS, RANGE_EPS = 1e-12, 1e-05
COMM = True

DOC_ORDER = (2, 1, 3, 0)
CTX_SLOT = (3, 2, 1)

STEPS = {
    "u00": (("x1", 0, 0), ("x1", 1, 0), ("x1", 2, 0), ("x1", 3, 0), ("x1", 4, 0), ("n0", 0, 0),),
    "q1": (("a1", 0, 0), ("x2", 0, 0), ("x1", 5, 0), ("x1", 6, 0), ("x1", 7, 0),),
    "u10": (("a1", 1, 0), ("a1", 2, 0), ("n1", 0, 0), ("x2", 2, 0),),
    "u11": (("a1", 3, 0),),
    "q2": (("a2", 0, 0), ("a1", 4, 0), ("x2", 4, 0), ("x2", 1, 0),),
    "u20": (("a2", 1, 0), ("a2", 2, 0),),
    "q3": (("a1", 0, 1), ("co", 0, 0), ("a2", 3, 0), ("n2", 0, 0), ("x1", 8, 0),),
    "u30": (("a2", 4, 0), ("a1", 5, 0), ("x2", 5, 0),),
    "u31": (("a2", 0, 1), ("a1", 6, 0), ("co", 1, 0), ("co", 2, 0), ("n3", 0, 0),),
    "o0": (("a1", 7, 0), ("a1", 2, 1), ("co", 3, 0), ("co", 4, 0),),
    "o1": (("co", 0, 1), ("a2", 5, 0), ("x2", 3, 0), ("x2", 7, 0), ("a2", 6, 0), ("a2", 7, 0), ("a1", 4, 1), ("a2", 2, 1),),
    "f00": (("a1", 8, 0), ("a1", 1, 1), ("co", 5, 0), ("co", 6, 0), ("x2", 8, 0),),
    "f01": (("a1", 5, 1), ("co", 7, 0), ("x2", 6, 0),),
    "f10": (("a2", 4, 1), ("a1", 3, 1), ("co", 2, 1),),
    "f11": (("a1", 7, 1),),
    "g00": (("a2", 8, 0), ("a1", 8, 1),),
    "g01": (("a2", 1, 1), ("a1", 6, 1),),
    "g10": (("a2", 5, 1), ("co", 4, 1),),
    "g11": (("a2", 3, 1),),
    "g20": (("a2", 7, 1),),
    "g21": (("co", 8, 0),),
    "g30": (("a2", 8, 1), ("co", 1, 1), ("a2", 6, 1), ("co", 5, 1), ("co", 3, 1), ("co", 7, 1),),
    "h00": (("co", 8, 1), ("co", 6, 1),),
}
STEPS_OF = {ev: n for n, ev in enumerate(e for evs in STEPS.values() for e in evs)}


def norm_rows(values, gain):
    center = jnp.mean(values, -1, keepdims=True)
    shifted = values - center
    spread = jnp.mean(shifted * shifted, -1, keepdims=True)
    return shifted * lax.rsqrt(spread + NORM_EPS) * gain


def gelu(v):
    return 0.5 * v * (1.0 + lax.erf(v * 0.7071067811865476))


def mm(a, b):
    return jnp.dot(a, b, preferred_element_type=jnp.float32)


def mm_rows(a, b):
    return lax.dot_general(a, b, (((0,), (0,)), ((), ())), preferred_element_type=jnp.float32)


def kernel(
    lens,
    states,
    w_in,
    w_out,
    gain1,
    w_up,
    w_down,
    gain2,
    cents,
    asg,
    places,
    res_o,
    ext_o,
    st,
    win,
    wout,
    up,
    down,
    cen,
    qs,
    ks,
    vs,
    cs,
    cr,
    hid,
    acc,
    nb0,
    nz,
    ny0,
    ny,
    nc0,
    nc,
    nx0,
    nx,
    es,
    er,
    lsem,
    wsem,
    ssem,
    rsem,
    asem,
    psem,
    s2sem,
    csem,
    nsem,
    esem,
):
    dp = lax.axis_index("dp")
    x = lax.axis_index("mp")
    c = lax.rem(dp, 2)
    y = lax.rem(dp // 2, 4)
    z = dp // 8

    def dev(x_, y_, z_, c_):
        return ((z_ * 4 + y_) * 2 + c_, x_)

    def plus(v, d):
        return lax.rem(v + (d + 4), 4)

    near_by = {
        (a, d): dev(*(plus(v, d) if n == a else v for n, v in (("x", x), ("y", y), ("z", z))), c)
        for a in "xyz"
        for d in (1, -1)
    }

    def peer(axis, d):
        if (axis, d) in near_by:
            return near_by[axis, d]
        if axis == "x":
            return dev(plus(x, d), y, z, c)
        if axis == "y":
            return dev(x, plus(y, d), z, c)
        if axis == "z":
            return dev(x, y, plus(z, d), c)
        return dev(x, y, z, 1 - c)

    def group(stage, n):
        if stage == 0:
            return dev(plus(x, n // 2), y, z, lax.rem(c + n, 2))
        return peer("xyz"[stage], n)

    def remote(src, dst, send, recv, to):
        return pltpu.make_async_remote_copy(
            src_ref=src, dst_ref=dst, send_sem=send, recv_sem=recv, device_id=to, device_id_type=MESH
        )

    def turn(i):
        return lax.rem(x + (2 + 3 * i + 3 * (i // 2) + 2 * (i // 3)), 4)

    def load_doc(i):
        return pltpu.make_async_copy(states.at[turn(i)], st.at[i], lsem.at[i])

    load_win = pltpu.make_async_copy(w_in, win, lsem.at[4])
    load_wout = pltpu.make_async_copy(w_out, wout.at[0], lsem.at[5])
    load_up = [
        pltpu.make_async_copy(
            w_up.at[:, pl.ds(j * UNITS, UNITS)], up.at[0, j], lsem.at[8 + j]
        )
        for j in range(CUTS)
    ]
    load_down = [
        pltpu.make_async_copy(
            w_down.at[pl.ds(j * UNITS, UNITS), :], down.at[0, j], lsem.at[8 + CUTS + j]
        )
        for j in range(CUTS)
    ]
    load_cen = pltpu.make_async_copy(cents, cen, lsem.at[6])
    load_doc(0).start()
    load_win.start()
    load_cen.start()
    for i in range(1, 4):
        load_doc(i).start()
    load_wout.start()
    for j in range(CUTS):
        load_up[j].start()
        load_down[j].start()

    def chunk(k):
        if k == 0:
            return wout, (), w_out, 0, 0, 16, WIDTH
        j = (k - 1) // 2
        if k % 2:
            return up, (j,), w_up, 0, j * UNITS, 64, UNITS
        return down, (j,), w_down, j * UNITS, 0, 16, WIDTH

    def rows(k, cc, color, q, n=1):
        size = chunk(k)[5]
        start = cc * (8 * size) + color * (4 * size) + q * size
        return pl.ds(pl.multiple_of(start, size), n * size)

    def place(k, r, rws, cols=slice(None)):
        buf, mid = chunk(k)[:2]
        return buf.at[(r,) + mid + (rws, cols)]

    def mine(color):
        return y if color == 0 else z

    def step_x1(k, color, d):
        _, _, src, row0, col0, size, ncols = chunk(k)
        start = row0 + c * (8 * size) + color * (4 * size) + mine(color) * size
        piece = src.at[pl.ds(pl.multiple_of(start, size), size), pl.ds(col0, ncols)]
        dst = place(k, 2 if d > 0 else 1, rows(k, c, color, mine(color)))
        n = color * 2 + (0 if d > 0 else 1)
        return remote(piece, dst, wsem.at[k, n], ssem.at[k, n], peer("x", d))

    def step_x2(k, color):
        d = 1 if color == 0 else -1
        rws = rows(k, c, color, mine(color))
        return remote(
            place(k, 2 if d > 0 else 1, rws),
            place(k, 3, rws),
            wsem.at[k, 4 + color],
            ssem.at[k, 4 + color],
            peer("x", d),
        )

    def span(p):
        return pl.ds(1, 2) if p == 0 else pl.ds(3, 1)

    def step_a1(k, p, color, d, arriving=False):
        q = plus(mine(color), -d) if arriving else mine(color)
        part = place(k, span(p), rows(k, c, color, q))
        n = color * 4 + (0 if d > 0 else 1)
        return remote(
            part, part, asem.at[k, p, n], rsem.at[k, p, n], peer("yz"[color], d)
        )

    def step_a2(k, p, color, d, arriving=False):
        q = plus(mine(color), -2 * d if arriving else -d)
        size, ncols = chunk(k)[5:]
        half = 0 if d > 0 else 1
        if size >= 32:
            start = c * (8 * size) + color * (4 * size) + q * size + half * (size // 2)
            part = place(k, span(p), pl.ds(pl.multiple_of(start, size // 2), size // 2))
        else:
            part = place(
                k, span(p), rows(k, c, color, q), pl.ds(half * (ncols // 2), ncols // 2)
            )
        n = color * 4 + 2 + half
        return remote(
            part, part, asem.at[k, p, n], rsem.at[k, p, n], peer("yz"[color], d)
        )

    def step_co(k, p, color, arriving=False):
        part = place(k, span(p), rows(k, 1 - c if arriving else c, 0, 0, 8))
        return remote(part, part, s2sem.at[k, p, color], psem.at[k, p, color], peer("c", 1))

    both = [(color, d) for color in range(2) for d in (1, -1)]

    def near_z(d):
        rws = pl.ds(pl.multiple_of(plus(z, d) * 32, 32), 32)
        return remote(nb0.at[rws, :], nz.at[d - 1], nsem.at[0, 0, d - 1], nsem.at[1, 0, d - 1], peer("z", d))

    def near_y(d):
        rws = pl.ds(pl.multiple_of(plus(y, d) * 8, 8), 8)
        return remote(ny0.at[rws, :], ny.at[d - 1], nsem.at[0, 1, d - 1], nsem.at[1, 1, d - 1], peer("y", d))

    def near_c():
        return remote(nc0, nc, nsem.at[0, 2, 0], nsem.at[1, 2, 0], peer("c", 1))

    def near_x(d):
        return remote(nx0, nx.at[d - 1], nsem.at[0, 3, d - 1], nsem.at[1, 3, d - 1], peer("x", d))

    def near_first():
        load_cen.wait()
        ids = asg[...]
        hi = ids // 128
        lo = ids - hi * 128
        slots = lax.broadcasted_iota(jnp.int32, (512, 128), 0)
        pick_hi = (hi == slots).astype(jnp.float32).astype(jnp.bfloat16)
        table = places[...]
        high = table // 256
        low = table - high * 256
        found = (
            mm_rows(high.astype(jnp.float32).astype(jnp.bfloat16), pick_hi) * 256.0
            + mm_rows(low.astype(jnp.float32).astype(jnp.bfloat16), pick_hi)
        )
        lanes = lax.broadcasted_iota(jnp.int32, (128, 128), 0)
        slot = jnp.sum(jnp.where(lanes == lo, found, 0.0), 0, keepdims=True)
        first = ((dp * 4 + x) * 512).astype(jnp.float32)
        picker = (slot - first == slots.astype(jnp.float32)).astype(jnp.float32).astype(jnp.bfloat16)
        nb0[...] = mm_rows(picker, cen[...]).astype(jnp.bfloat16)

    def event(kind, k, p):
        if kind == "x1":
            for color, d in both:
                step_x1(k, color, d).start()
        elif kind == "x2":
            before = STEPS_OF[("x2", k, 0)] < STEPS_OF[("a1", k, 0)]
            for color, d in ((0, 1), (1, -1)):
                if before:
                    step_x1(k, color, d).wait_recv()
                step_x2(k, color).start()
        elif kind == "a1":
            if p == 0:
                step_x1(k, 0, -1).wait_recv()
                step_x1(k, 1, 1).wait_recv()
                if STEPS_OF[("x2", k, 0)] > STEPS_OF[("a1", k, 0)]:
                    step_x1(k, 0, 1).wait_recv()
                    step_x1(k, 1, -1).wait_recv()
            else:
                for color in range(2):
                    step_x2(k, color).wait_recv()
            for color, d in both:
                step_a1(k, p, color, d).start()
        elif kind == "a2":
            for color, d in both:
                step_a1(k, p, color, d, True).wait_recv()
                step_a2(k, p, color, d).start()
        elif kind == "co":
            for color, d in both:
                step_a2(k, p, color, d, True).wait_recv()
            step_co(k, p, 0).start()
        elif kind == "n0":
            near_first()
            for d in (1, 2, 3):
                near_z(d).start()
        elif kind == "n1":
            total = nb0[pl.ds(pl.multiple_of(z * 32, 32), 32), :].astype(jnp.float32)
            for d in (1, 2, 3):
                near_z(d).wait_recv()
                total += nz[d - 1].astype(jnp.float32)
            ny0[...] = total
            for d in (1, 2, 3):
                near_y(d).start()
        elif kind == "n2":
            total = ny0[pl.ds(pl.multiple_of(y * 8, 8), 8), :]
            for d in (1, 2, 3):
                near_y(d).wait_recv()
                total += ny[d - 1]
            nc0[...] = total
            near_c().start()
        elif kind == "n3":
            near_c().wait_recv()
            nx0[...] = nc0[...] + nc[...]
            for d in (1, 2, 3):
                near_x(d).start()

    def flush(tau):
        if COMM:
            for kind, k, p in STEPS.get(tau, ()):
                event(kind, k, p)

    def in_loop(i, slot):
        for ii in range(4):
            tau = f"q{ii + 1}" if slot == 2 else f"u{ii}{slot}"
            if STEPS.get(tau):

                @pl.when(i == ii)
                def _():
                    flush(tau)

    def send_ctx(i, p):
        cols = pl.ds(p * 128, 128)
        return remote(
            cs.at[i, :, cols],
            cr.at[CTX_SLOT[i], :, cols],
            csem.at[0, i, p],
            csem.at[1, i, p],
            peer("x", DOC_ORDER[i]),
        )

    if COMM:
        barrier = pltpu.get_barrier_semaphore()
        peers = [group(0, n) for n in range(1, 8)] + [peer(a, d) for a in "yz" for d in (1, 2, 3)]
        for p in peers:
            pl.semaphore_signal(barrier, inc=1, device_id=p, device_id_type=MESH)

    lane = lax.broadcasted_iota(jnp.int32, (SEQ // QB, 128), 1) < 64
    lane_all = lax.broadcasted_iota(jnp.int32, (SEQ, 128), 1) < 64

    def project(i):
        load_doc(i).wait()
        doc = st[i]
        q32 = mm(doc, win[0]) * 0.125
        for p in range(2):
            part = q32[:, p * 128 : p * 128 + 128]
            qs[2 * p] = jnp.where(lane_all, part, 0.0).astype(jnp.bfloat16)
            qs[2 * p + 1] = jnp.where(lane_all, 0.0, part).astype(jnp.bfloat16)
        ks[...] = mm(doc, win[1]).astype(jnp.bfloat16)
        v32 = mm(doc, win[2])
        for p in range(2):
            part = v32[:, p * 128 : p * 128 + 128]
            vs[2 * p] = jnp.where(lane_all, part, 1.0).astype(jnp.bfloat16)
            vs[2 * p + 1] = jnp.where(lane_all, 1.0, part).astype(jnp.bfloat16)
    load_win.wait()
    project(0)
    if COMM:
        pl.semaphore_wait(barrier, len(peers))

    @pl.loop(0, 4)
    def _(i):
        bias = jnp.where(
            lax.broadcasted_iota(jnp.int32, (1, SEQ), 1) < lens[turn(i)], 0.0, -1e30
        )
        for p in range(2):
            in_loop(i, p)
            keys = ks[:, p * 128 : p * 128 + 128]
            for qb in range(QB):
                outs = []
                rws = pl.ds(qb * (SEQ // QB), SEQ // QB)
                for h in range(2):
                    scores = lax.dot_general(
                        qs[2 * p + h, rws],
                        keys,
                        (((1,), (1,)), ((), ())),
                        preferred_element_type=jnp.float32,
                    )
                    scores = scores + bias
                    e = jnp.exp(scores - jnp.max(scores, -1, keepdims=True)).astype(jnp.bfloat16)
                    outs.append(mm(e, vs[2 * p + h]))
                top = jnp.where(lane, outs[0], outs[1])
                mass = pltpu.roll(jnp.where(lane, outs[1], outs[0]), 64, 1)
                cs[i, rws, p * 128 : p * 128 + 128] = (top / mass).astype(jnp.bfloat16)
            if COMM:
                for ii in range(3):

                    @pl.when(i == ii)
                    def _():
                        send_ctx(ii, p).start()

        in_loop(i, 2)

        @pl.when(i < 3)
        def _():
            project(i + 1)

    def arrive(k, p):
        if COMM:
            step_co(k, p, 0, True).wait_recv()

    flush("o0")
    load_wout.wait()
    acc[...] = st[3].astype(jnp.float32) + mm(cs[3], wout[0])
    flush("o1")
    arrive(0, 0)
    arrive(0, 1)
    if COMM:
        for i in range(3):
            for p in range(2):
                send_ctx(i, p).wait_recv()
    part = mm(cr[1], wout[1]) + mm(cr[2], wout[2]) + mm(cr[3], wout[3])
    hidden = norm_rows(acc[...] + part, gain1[...])
    hid[...] = hidden.astype(jnp.bfloat16)
    acc[...] = hid[...].astype(jnp.float32)

    def ffn(parts, between):
        for mb in range(2):
            if mb:
                flush(between)
            rws = pl.ds(mb * 256, 256)
            h = hid[rws, :]
            total = acc[rws, :]
            for r, j in parts:
                act = gelu(mm(h, up[r, j])).astype(jnp.bfloat16)
                total += mm(act, down[r, j])
            acc[rws, :] = total

    for n in range(CUTS // 2):
        flush(f"f{n}0")
        for j in (2 * n, 2 * n + 1):
            load_up[j].wait()
            load_down[j].wait()
        ffn(((0, 2 * n), (0, 2 * n + 1)), f"f{n}1")
    for j in range(CUTS):
        flush(f"g{j}0")
        arrive(1 + 2 * j, 0)
        arrive(2 + 2 * j, 0)
        ffn(((1, j), (2, j)), f"g{j}1")
    for n in range(CUTS // 2):
        flush(f"h{n}0")
        for k in range(1 + 4 * n, 5 + 4 * n):
            arrive(k, 1)
        ffn(((3, 2 * n), (3, 2 * n + 1)), f"h{n}1")
    flush("end")

    normed = norm_rows(acc[...], gain2[...])
    own_len = lens[x]
    live = lax.broadcasted_iota(jnp.int32, (SEQ, 1), 0) < own_len
    pooled = jnp.sum(jnp.where(live, normed, 0.0), 0, keepdims=True) / own_len.astype(jnp.float32)
    near = nx0[...]
    if COMM:
        for d in (1, 2, 3):
            near_x(d).wait_recv()
            near += nx[d - 1]
    mark = lax.broadcasted_iota(jnp.int32, (8, 1), 0) == c * 4 + x
    near = jnp.sum(jnp.where(mark, near, 0.0), 0, keepdims=True)
    flat = pooled - near
    for j in range(8):
        es[0, 0, j : j + 1, :] = flat[:, j * 128 : j * 128 + 128]
    residual = es[0, 0]
    es[0, 1] = -residual

    def extreme(stage, n):
        return remote(
            es.at[stage], er.at[stage, n - 1], esem.at[0, stage, n - 1], esem.at[1, stage, n - 1],
            group(stage, n),
        )

    def reach(stage):
        return range(1, 8 if stage == 0 else 4)

    def sent(k):
        for color, d in both:
            step_x1(k, color, d).wait_send()
            for p in range(2):
                step_a1(k, p, color, d).wait_send()
                step_a2(k, p, color, d).wait_send()
        for color in range(2):
            step_x2(k, color).wait_send()
        for p in range(2):
            step_co(k, p, 0).wait_send()

    best = jnp.concatenate([es[0, 0][None], es[0, 1][None]], 0)
    if COMM:
        for stage in range(3):
            if stage:
                es[stage] = best
            for d in reach(stage):
                extreme(stage, d).start()
            for k in range(3 * stage, 3 * stage + 3):
                sent(k)
            for d in reach(stage):
                extreme(stage, d).wait_recv()
                best = jnp.maximum(best, er[stage, d - 1])
    res_o[...] = residual
    ext_o[...] = best

    if COMM:
        for d in (1, 2, 3):
            near_z(d).wait_send()
            near_y(d).wait_send()
            near_x(d).wait_send()
        near_c().wait_send()
        for i in range(3):
            for p in range(2):
                send_ctx(i, p).wait_send()
        for stage in range(3):
            for d in reach(stage):
                extreme(stage, d).wait_send()
    else:
        load_cen.wait()


def finish(res, ext, codes_o, lower_o, upper_o):
    upper = ext[0]
    lower = -ext[1]
    upper_o[...] = upper
    lower_o[...] = lower
    codes_o[...] = (res[...] - lower) / (upper - lower + RANGE_EPS)


def body(
    states,
    lengths,
    attn_in,
    attn_out,
    attn_gain,
    ffn_up,
    ffn_down,
    ffn_gain,
    centroids,
    assignment,
    list_place,
):
    hbm = pl.BlockSpec(memory_space=pl.ANY)
    vmem = pl.BlockSpec(memory_space=pltpu.VMEM)
    smem = pl.BlockSpec(memory_space=pltpu.SMEM)
    bf, f32 = jnp.bfloat16, jnp.float32
    tile = jax.ShapeDtypeStruct((8, 128), f32)
    dma = pltpu.SemaphoreType.DMA
    residual, extremes = pl.pallas_call(
        kernel,
        out_shape=(tile, jax.ShapeDtypeStruct((2, 8, 128), f32)),
        in_specs=[smem, hbm, hbm, hbm, vmem, hbm, hbm, vmem, hbm, vmem, vmem],
        out_specs=(vmem, vmem),
        scratch_shapes=[
            pltpu.VMEM((4, SEQ, WIDTH), bf),
            pltpu.VMEM((3, WIDTH, GROUP), bf),
            pltpu.VMEM((4, GROUP, WIDTH), bf),
            pltpu.VMEM((4, CUTS, WIDTH, UNITS), bf),
            pltpu.VMEM((4, CUTS, UNITS, WIDTH), bf),
            pltpu.VMEM((512, WIDTH), bf),
            pltpu.VMEM((4, SEQ, 128), bf),
            pltpu.VMEM((SEQ, GROUP), bf),
            pltpu.VMEM((4, SEQ, 128), bf),
            pltpu.VMEM((4, SEQ, GROUP), bf),
            pltpu.VMEM((4, SEQ, GROUP), bf),
            pltpu.VMEM((SEQ, WIDTH), bf),
            pltpu.VMEM((SEQ, WIDTH), f32),
            pltpu.VMEM((128, WIDTH), bf),
            pltpu.VMEM((3, 32, WIDTH), bf),
            pltpu.VMEM((32, WIDTH), f32),
            pltpu.VMEM((3, 8, WIDTH), f32),
            pltpu.VMEM((8, WIDTH), f32),
            pltpu.VMEM((8, WIDTH), f32),
            pltpu.VMEM((8, WIDTH), f32),
            pltpu.VMEM((3, 8, WIDTH), f32),
            pltpu.VMEM((3, 2, 8, 128), f32),
            pltpu.VMEM((3, 7, 2, 8, 128), f32),
            dma((8 + 2 * CUTS,)),
            dma((CHUNKS, 6)),
            dma((CHUNKS, 6)),
            dma((CHUNKS, 2, 8)),
            dma((CHUNKS, 2, 8)),
            dma((CHUNKS, 2, 1)),
            dma((CHUNKS, 2, 1)),
            dma((2, 3, 2)),
            dma((2, 4, 3)),
            dma((2, 3, 7)),
        ],
        compiler_params=pltpu.CompilerParams(
            vmem_limit_bytes=60 * 2**20,
            **(dict(collective_id=0, has_side_effects=True) if COMM else {}),
        ),
        name="encode",
    )(
        lengths,
        states,
        attn_in,
        attn_out,
        attn_gain.reshape(1, WIDTH),
        ffn_up,
        ffn_down,
        ffn_gain.reshape(1, WIDTH),
        centroids,
        assignment.reshape(1, 128),
        list_place.reshape(512, 128),
    )
    codes, lower, upper = pl.pallas_call(
        finish,
        out_shape=(tile, tile, tile),
        in_specs=[vmem, vmem],
        out_specs=(vmem, vmem, vmem),
        name="finish",
    )(residual, extremes)
    return codes.reshape(1, WIDTH), lower.reshape(WIDTH), upper.reshape(WIDTH)


def solution(mesh):
    placed = (
        P("dp", None, None),
        P("dp"),
        P(None, None, "mp"),
        P("mp", None),
        P(),
        P(None, "mp"),
        P("mp", None),
        P(),
        P(("dp", "mp"), None),
        P(),
        P(),
    )
    return jax.shard_map(
        body,
        mesh=mesh,
        in_specs=placed,
        out_specs=(P(("dp", "mp"), None), P(), P()),
        check_vma=False,
    )
```
